32 devices in a mesh: pix: 16 (over z, y, x), lat: 2 (over core).
Axes of the slice: x: 2, y: 2, z: 4, core: 2. Of those that a mesh axis runs over, the one named last changes fastest.
Arguments:
- latents: bfloat16 [8192, 512], P('pix'), may hold values from -6 to 6
- w_send: bfloat16 [512, 512], P(None, 'lat'), may hold values from -0.25 to 0.25
- w_recv: bfloat16 [512, 512], P(None, 'lat'), may hold values from -0.25 to 0.25
- edge_bias: float32 [512], P('lat'), may hold values from -3 to 3
- w_msg: bfloat16 [512, 512], P('lat'), may hold values from -0.25 to 0.25
- w_self: bfloat16 [512, 512], P(None, 'lat'), may hold values from -0.25 to 0.25
- w_agg: bfloat16 [512, 512], P(None, 'lat'), may hold values from -0.25 to 0.25
- node_bias: float32 [512], P('lat'), may hold values from -3 to 3
- w_node: bfloat16 [512, 512], P('lat'), may hold values from -0.25 to 0.25
- norm_gain: float32 [512], replicated, may hold values from 0.25 to 1.75
- coarse_ids: int32 [128], P('pix'), may hold values from 0 to 511
- send_list: int32 [16], P('pix'), may hold values from 0 to 3
- recv_tile: int32 [512], P('pix'), may hold values from 0 to 3
- send_tile: int32 [512], P('pix'), may hold values from 0 to 6, as said below
- edge_ends: int32 [512, 2, 128], P('pix'), may hold values from 0 to 127
- edge_mask: int32 [512, 128], P('pix'), may hold values 0 or 1
- cotangent: bfloat16 [8192, 512], P('pix'), may hold values from -6 to 6
Outputs:
- new_latents: bfloat16 [8192, 512], P('pix')
- grad_latents: float32 [8192, 512], P('pix', 'lat')
- grad_w_send: float32 [512, 512], P(None, 'lat')
- grad_w_recv: float32 [512, 512], P(None, 'lat')
- grad_edge_bias: float32 [512], P('lat')
- grad_w_msg: float32 [512, 512], P('lat')
- grad_w_self: float32 [512, 512], P(None, 'lat')
- grad_w_agg: float32 [512, 512], P(None, 'lat')
- grad_node_bias: float32 [512], P('lat')
- grad_w_node: float32 [512, 512], P('lat')
- grad_gain: float32 [512], replicated
The draws below stay inside these ranges and needn't reach their ends.
Inputs may be any that keep to these rules, and one draw needn't show every extreme that they name: `send_tile`: a block's sender tile, numbered as in the first step: first the device's own tiles, then the 1 lent tiles of the preceding and of the following pixel range, then the 1 tiles of the coarse panel; in each device's own run of 32 blocks, the first names a tile lent by the preceding range and the second one lent by the following range. `coarse_ids`: rows may repeat.
All inputs are finite; a program needn't handle non-finite values. No bound on the sum of `edge_mask` on one device may be relied on, other than what follows from the above.
Results may differ from the reference program's by a relative error of at most 0.0085.
Values may be sent and summed in bfloat16 or wider, within the bound.
A program may use at most 128 MiB of HBM per device.

```python
import math
import jax
import jax.numpy as jnp
from jax import lax

LATENT = 512
HIDDEN_SIZE = 512
TILE = 128
TILES_DEV = 4
HALO_T = 1
COARSE_DEV = 8
NODE_DEV = 512
NODES = 8192
BLOCKS_DEV = 32
BLOCKS = 512
COARSE = 128
PANEL_TILES = 1
N_PIX = 16


def draw_send_tile(key, part):
    key_kind, key_local, key_side, key_panel, key_left, key_right = jax.random.split(key, 6)
    choose_kind = jax.random.randint(key_kind, (BLOCKS,), 0, 10)
    local_tile = jax.random.randint(key_local, (BLOCKS,), 0, TILES_DEV)
    side_slot = jax.random.randint(key_side, (BLOCKS,), 0, 2 * HALO_T)
    panel_tile = jax.random.randint(key_panel, (BLOCKS,), 0, PANEL_TILES)
    left_slot = jax.random.randint(key_left, (BLOCKS,), 0, HALO_T)
    right_slot = jax.random.randint(key_right, (BLOCKS,), 0, HALO_T)
    picked = jnp.where(choose_kind < 5, local_tile, jnp.where(choose_kind < 7, TILES_DEV + side_slot, TILES_DEV + 2 * HALO_T + panel_tile))
    position = jnp.arange(BLOCKS, dtype=jnp.int32) % BLOCKS_DEV
    picked = jnp.where(position == 0, TILES_DEV + left_slot, jnp.where(position == 1, TILES_DEV + HALO_T + right_slot, picked))
    return picked.astype(jnp.int32)


def touch_ends(result, key, smallest, top_value):
    longest = result.shape.index(max(result.shape))
    spots = []
    for shift in (0, 1):
        where = [jax.random.randint(jax.random.fold_in(key, axis), (), 0, length) for axis, length in enumerate(result.shape)]
        where[longest] = (where[longest] + shift) % result.shape[longest]
        spots.append(tuple(where))
    return result.at[spots[0]].set(smallest).at[spots[1]].set(top_value)


def level_of(rng, extent, shards, smallest, high):
    level = 1.0
    for dim, parts in shards:
        steps = jax.random.uniform(jax.random.fold_in(jax.random.fold_in(rng, 6), dim), (parts,), jnp.float32, smallest / len(shards), high / len(shards))
        level = level * jnp.repeat(jnp.exp(steps), extent[dim] // parts).reshape((-1,) + (1,) * (len(extent) - 1 - dim))
    return level


def centred(stream_key, dims, width, reach, pieces=(), kind=jnp.bfloat16):
    array = width * jax.random.normal(stream_key, dims, jnp.float32)
    if pieces:
        array = array * level_of(stream_key, dims, pieces, -0.22, 0.18)
    return jnp.clip(array, -reach, reach).astype(kind)


def setup_inputs(seed: int = 0) -> dict:
    streams_of = jax.random.split(jax.random.key(seed), 18)
    latents = centred(streams_of[0], (NODES, LATENT), 1.0, 6.0, ((0, 16),))
    w_send = centred(streams_of[1], (LATENT, HIDDEN_SIZE), LATENT ** -0.5, 0.25, ((1, 2),))
    w_recv = centred(streams_of[2], (LATENT, HIDDEN_SIZE), LATENT ** -0.5, 0.25, ((1, 2),))
    edge_bias = centred(streams_of[3], (HIDDEN_SIZE,), 0.5, 3.0, ((0, 2),), jnp.float32)
    w_msg = centred(streams_of[4], (HIDDEN_SIZE, LATENT), HIDDEN_SIZE ** -0.5, 0.25, ((0, 2),))
    w_self = centred(streams_of[5], (LATENT, HIDDEN_SIZE), LATENT ** -0.5, 0.25, ((1, 2),))
    w_agg = centred(streams_of[6], (LATENT, HIDDEN_SIZE), LATENT ** -0.5, 0.25, ((1, 2),))
    node_bias = centred(streams_of[7], (HIDDEN_SIZE,), 0.5, 3.0, ((0, 2),), jnp.float32)
    w_node = centred(streams_of[8], (HIDDEN_SIZE, LATENT), HIDDEN_SIZE ** -0.5, 0.25, ((0, 2),))
    norm_gain = jnp.clip(1.0 + 0.15 * jax.random.normal(streams_of[9], (LATENT,), jnp.float32), 0.25, 1.75)
    coarse_ids = touch_ends(jax.random.randint(streams_of[10], (COARSE,), 0, NODE_DEV), jax.random.fold_in(streams_of[10], 1), 0, NODE_DEV - 1).astype(jnp.int32)
    send_list = touch_ends(jax.random.randint(streams_of[11], (HALO_T * N_PIX,), 0, TILES_DEV), jax.random.fold_in(streams_of[11], 1), 0, TILES_DEV - 1).astype(jnp.int32)
    recv_tile = touch_ends(jax.random.randint(streams_of[12], (BLOCKS,), 0, TILES_DEV), jax.random.fold_in(streams_of[12], 1), 0, TILES_DEV - 1).astype(jnp.int32)
    send_tile = draw_send_tile(jax.random.fold_in(streams_of[17], 71), 0)
    edge_ends = touch_ends(jax.random.randint(streams_of[14], (BLOCKS, 2, TILE), 0, TILE), jax.random.fold_in(streams_of[14], 1), 0, TILE - 1).astype(jnp.int32)
    edge_mask = touch_ends((jax.random.randint(streams_of[15], (BLOCKS, TILE), 0, 4) < 3).astype(jnp.int32), jax.random.fold_in(streams_of[15], 1), 0, 1)
    cotangent = centred(streams_of[16], (NODES, LATENT), 1.0, 6.0, ((0, 16),))
    return {"latents": latents, "w_send": w_send, "w_recv": w_recv, "edge_bias": edge_bias, "w_msg": w_msg, "w_self": w_self, "w_agg": w_agg, "node_bias": node_bias, "w_node": w_node, "norm_gain": norm_gain, "coarse_ids": coarse_ids, "send_list": send_list, "recv_tile": recv_tile, "send_tile": send_tile, "edge_ends": edge_ends, "edge_mask": edge_mask, "cotangent": cotangent}


norm_eps = 1e-05

def silu_slope(values):
    sigma = jax.nn.sigmoid(values)
    return sigma * (1.0 + values * (1.0 - sigma))

def reference(latents, w_send, w_recv, edge_bias, w_msg, w_self, w_agg, node_bias, w_node, norm_gain, coarse_ids, send_list, recv_tile, send_tile, edge_ends, edge_mask, cotangent):
    block_ids = jnp.arange(BLOCKS, dtype=jnp.int32)
    owner_dev = block_ids // BLOCKS_DEV
    left_dev = (owner_dev + N_PIX - 1) % N_PIX
    right_dev = (owner_dev + 1) % N_PIX
    sender_offs = edge_ends[:, 0, :]
    left_slot = jnp.clip(send_tile - TILES_DEV, 0, HALO_T - 1)
    right_slot = jnp.clip(send_tile - TILES_DEV - HALO_T, 0, HALO_T - 1)
    left_tile = send_list[left_dev * HALO_T + left_slot]
    right_tile = send_list[right_dev * HALO_T + right_slot]
    panel_slot = jnp.clip(send_tile - TILES_DEV - 2 * HALO_T, 0, PANEL_TILES - 1)
    panel_pos = panel_slot[:, None] * TILE + sender_offs
    panel_node = panel_pos // COARSE_DEV * NODE_DEV + coarse_ids[panel_pos]
    local_node = owner_dev[:, None] * NODE_DEV + send_tile[:, None] * TILE + sender_offs
    left_node = left_dev[:, None] * NODE_DEV + left_tile[:, None] * TILE + sender_offs
    right_node = right_dev[:, None] * NODE_DEV + right_tile[:, None] * TILE + sender_offs
    kinds = send_tile[:, None]
    senders = jnp.where(kinds < TILES_DEV, local_node, jnp.where(kinds < TILES_DEV + HALO_T, left_node, jnp.where(kinds < TILES_DEV + 2 * HALO_T, right_node, panel_node)))
    receivers = owner_dev[:, None] * NODE_DEV + recv_tile[:, None] * TILE + edge_ends[:, 1, :]
    edges_dev = BLOCKS_DEV * TILE
    senders = senders.reshape(N_PIX, edges_dev).astype(jnp.int32)
    receivers = receivers.reshape(N_PIX, edges_dev).astype(jnp.int32)
    edge_weight = edge_mask.astype(jnp.float32).reshape(N_PIX, edges_dev)
    device_ids = jnp.arange(N_PIX, dtype=jnp.int32)
    send_proj = jnp.dot(latents, w_send, preferred_element_type=jnp.float32)
    recv_proj = jnp.dot(latents, w_recv, preferred_element_type=jnp.float32)

    def edge_forward(edge_item):
        src_rows, dst_rows, weight_row, device = edge_item
        edge_pre = send_proj[src_rows] + recv_proj[dst_rows] + edge_bias
        edge_act = jax.nn.silu(edge_pre).astype(jnp.bfloat16)
        message = jnp.dot(edge_act, w_msg, preferred_element_type=jnp.float32)
        return jax.ops.segment_sum(message * weight_row[:, None], dst_rows - device * NODE_DEV, num_segments=NODE_DEV)
    aggregate = lax.map(edge_forward, (senders, receivers, edge_weight, device_ids)).reshape(NODES, LATENT)
    aggregate_bf = aggregate.astype(jnp.bfloat16)
    node_pre = jnp.dot(latents, w_self, preferred_element_type=jnp.float32) + jnp.dot(aggregate_bf, w_agg, preferred_element_type=jnp.float32) + node_bias
    node_act = jax.nn.silu(node_pre).astype(jnp.bfloat16)
    node_out = jnp.dot(node_act, w_node, preferred_element_type=jnp.float32)
    row_mean = lax.optimization_barrier(jnp.mean(node_out, axis=-1, keepdims=True))
    centered = node_out - row_mean
    row_var = lax.optimization_barrier(jnp.mean(centered * centered, axis=-1, keepdims=True))
    inv_std = lax.rsqrt(row_var + norm_eps)
    normed = centered * inv_std
    new_latents = (latents.astype(jnp.float32) + normed * norm_gain).astype(jnp.bfloat16)
    grad_out = cotangent.astype(jnp.float32)
    gain_sum = lax.optimization_barrier(jnp.sum(grad_out * normed, axis=0))
    d_normed = grad_out * norm_gain
    out_cot = inv_std * (d_normed - lax.optimization_barrier(jnp.mean(d_normed, axis=-1, keepdims=True)) - normed * lax.optimization_barrier(jnp.mean(d_normed * normed, axis=-1, keepdims=True)))
    out_cot_bf = out_cot.astype(jnp.bfloat16)
    node_w_grad = jnp.dot(node_act.T, out_cot_bf, preferred_element_type=jnp.float32)
    node_pre_cot = jnp.dot(out_cot_bf, w_node.T, preferred_element_type=jnp.float32) * silu_slope(node_pre)
    node_bias_sum = lax.optimization_barrier(jnp.sum(node_pre_cot, axis=0))
    node_pre_bf = node_pre_cot.astype(jnp.bfloat16)
    self_w_grad = jnp.dot(latents.T, node_pre_bf, preferred_element_type=jnp.float32)
    agg_w_grad = jnp.dot(aggregate_bf.T, node_pre_bf, preferred_element_type=jnp.float32)
    self_cot = jnp.dot(node_pre_bf, w_self.T, preferred_element_type=jnp.float32)
    agg_cot = jnp.dot(node_pre_bf, w_agg.T, preferred_element_type=jnp.float32)
    agg_cot_bf = agg_cot.astype(jnp.bfloat16)

    def edge_backward(totals, edge_item):
        src_grad, msg_grad, bias_grad = totals
        src_rows, dst_rows, weight_row, device = edge_item
        edge_pre = send_proj[src_rows] + recv_proj[dst_rows] + edge_bias
        edge_act = jax.nn.silu(edge_pre).astype(jnp.bfloat16)
        msg_cot = agg_cot_bf[dst_rows] * weight_row.astype(jnp.bfloat16)[:, None]
        msg_grad = msg_grad + jnp.dot(edge_act.T, msg_cot, preferred_element_type=jnp.float32)
        pre_cot = jnp.dot(msg_cot, w_msg.T, preferred_element_type=jnp.float32) * silu_slope(edge_pre)
        bias_grad = bias_grad + lax.optimization_barrier(jnp.sum(pre_cot, axis=0))
        src_grad = src_grad.at[src_rows].add(pre_cot)
        dst_grad = jax.ops.segment_sum(pre_cot, dst_rows - device * NODE_DEV, num_segments=NODE_DEV)
        return ((src_grad, msg_grad, bias_grad), dst_grad)
    start_totals = (jnp.zeros((NODES, HIDDEN_SIZE), jnp.float32), jnp.zeros((HIDDEN_SIZE, LATENT), jnp.float32), jnp.zeros((HIDDEN_SIZE,), jnp.float32))
    (src_cot, msg_w_grad, edge_bias_sum), dst_cot = lax.scan(edge_backward, start_totals, (senders, receivers, edge_weight, device_ids))
    src_cot_bf = src_cot.astype(jnp.bfloat16)
    dst_cot_bf = dst_cot.reshape(NODES, HIDDEN_SIZE).astype(jnp.bfloat16)
    send_w_grad = jnp.dot(latents.T, src_cot_bf, preferred_element_type=jnp.float32)
    recv_w_grad = jnp.dot(latents.T, dst_cot_bf, preferred_element_type=jnp.float32)
    grad_latents = grad_out + self_cot + jnp.dot(src_cot_bf, w_send.T, preferred_element_type=jnp.float32) + jnp.dot(dst_cot_bf, w_recv.T, preferred_element_type=jnp.float32)
    grad_scale = 1.0 / math.sqrt(NODES)
    return (new_latents, grad_latents, grad_scale * send_w_grad, grad_scale * recv_w_grad, grad_scale * edge_bias_sum, grad_scale * msg_w_grad, grad_scale * self_w_grad, grad_scale * agg_w_grad, grad_scale * node_bias_sum, grad_scale * node_w_grad, grad_scale * gain_sum)
```

```python
import functools
import math

import jax
import jax.numpy as jnp
from jax import lax
from jax.experimental import pallas as pl
from jax.experimental.pallas import tpu as pltpu
from jax.sharding import PartitionSpec as P

norm_eps = 1e-05
f32 = jnp.float32
bf16 = jnp.bfloat16
MESH = pl.DeviceIdType.MESH
VM = pl.BlockSpec(memory_space=pltpu.VMEM)
SM = pl.BlockSpec(memory_space=pltpu.SMEM)
PLANE = 4
GROUPS = 2
LIMIT = 60 * 1024 * 1024


def dot(a, b):
    return jnp.dot(a, b, preferred_element_type=f32)


def dot_tn(a, b):
    return lax.dot_general(a, b, (((0,), (0,)), ((), ())), preferred_element_type=f32)


def dot_nt(a, b):
    return lax.dot_general(a, b, (((1,), (1,)), ((), ())), preferred_element_type=f32)


def sigmoid(v):
    return 0.5 * jnp.tanh(0.5 * v) + 0.5


def remote(src, dst, send, recv, where):
    return pltpu.make_async_remote_copy(
        src_ref=src, dst_ref=dst, send_sem=send, recv_sem=recv, device_id=where, device_id_type=MESH
    )


def enter(pix_count, partner):
    me = lax.axis_index("pix")
    barrier = pltpu.get_barrier_semaphore()
    total = 0
    for d in range(1, pix_count):
        to = lax.rem(me + d, pix_count)
        pl.semaphore_signal(barrier, inc=1, device_id={"pix": to}, device_id_type=MESH)
        total += 1
    if partner:
        other = 1 - lax.axis_index("lat")
        pl.semaphore_signal(barrier, inc=1, device_id={"lat": other}, device_id_type=MESH)
        total += 1
    pl.semaphore_wait(barrier, total)


def comm_call(body, outs, ins, scratch, cid, flops=10**8, byts=10**6):
    return pl.pallas_call(
        body,
        out_shape=outs,
        in_specs=ins,
        out_specs=[VM] * len(outs),
        scratch_shapes=scratch,
        compiler_params=pltpu.CompilerParams(
            collective_id=cid, has_side_effects=True, vmem_limit_bytes=LIMIT
        ),
        cost_estimate=pl.CostEstimate(flops=flops, bytes_accessed=byts, transcendentals=0),
    )


def share_kernel(
    n, lat_ref, lent_ref, coarse_ref, ws_ref, wr_ref, wm_ref, wn_ref, wa_ref,
    src_ref, rcv_ref, wm_out, wn_out, wa_out,
    halo, panel, wm, wn, wa, ssem, rsem, csend, crecv,
):
    me = lax.axis_index("pix")
    lat = lax.axis_index("lat")
    other = 1 - lat
    right = lax.rem(me + 1, n)
    left = lax.rem(me + n - 1, n)
    enter(n, True)
    copies = [
        remote(lent_ref, halo.at[0], ssem.at[0], rsem.at[0], {"pix": right}),
        remote(lent_ref, halo.at[1], ssem.at[1], rsem.at[1], {"pix": left}),
    ]
    for d in range(1, n):
        to = lax.rem(me + d, n)
        copies.append(remote(coarse_ref, panel.at[me], csend.at[d], crecv.at[d], {"pix": to}))
    part = wm_ref.shape[0]
    wcopies = [
        remote(wm_ref, wm.at[lat], ssem.at[2], rsem.at[2], {"lat": other}),
        remote(wn_ref, wn.at[lat], ssem.at[3], rsem.at[3], {"lat": other}),
        remote(wa_ref, wa.at[lat], ssem.at[4], rsem.at[4], {"lat": other}),
    ]
    for c in copies + wcopies:
        c.start()
    panel[me] = coarse_ref[...]
    wm[lat] = wm_ref[...]
    wn[lat] = wn_ref[...]
    wa[lat] = wa_ref[...]
    rows = lat_ref.shape[0]
    hrows = lent_ref.shape[0]
    src_ref[0:rows, :] = dot(lat_ref[...], ws_ref[...]).astype(bf16)
    rcv_ref[...] = dot(lat_ref[...], wr_ref[...]).astype(bf16)
    for c in copies:
        c.wait()
    for k in range(2):
        src_ref[rows + k * hrows : rows + (k + 1) * hrows, :] = dot(halo[k], ws_ref[...]).astype(bf16)
    base = rows + 2 * hrows
    prows = panel.shape[0] * panel.shape[1]
    flat = panel[...].astype(f32).reshape(prows, panel.shape[2]).astype(bf16)
    src_ref[base : base + prows, :] = dot(flat, ws_ref[...]).astype(bf16)
    for c in wcopies:
        c.wait()
    for k in range(2):
        wm_out[k * part : (k + 1) * part, :] = wm[k]
        wn_out[k * part : (k + 1) * part, :] = wn[k]
        wa_out[:, k * part : (k + 1) * part] = wa[k]


def one_hots(cols, t):
    lane = lax.broadcasted_iota(jnp.int32, (t, t), 1)
    return lane == cols


def edge_forward(st, rt, cols_ref, ends_ref, mask_ref, src_ref, rcv_ref, bias_ref, sum_ref, slope_ref):
    blocks, _, t = ends_ref.shape
    sum_ref[...] = jnp.zeros_like(sum_ref)
    lane = lax.broadcasted_iota(jnp.int32, (t, t), 1)
    sub = lax.broadcasted_iota(jnp.int32, (t, t), 0)
    bias = bias_ref[...]

    @pl.loop(0, blocks, unroll=4)
    def _(b):
        cols = cols_ref[b]
        oh = jnp.concatenate(
            [(cols[:, 0:1] == lane).astype(bf16), (cols[:, 1:2] == lane).astype(bf16)], axis=1
        )
        s0 = pl.multiple_of(st[b] * t, t)
        r0 = pl.multiple_of(rt[b] * t, t)
        both = jnp.concatenate([src_ref[pl.ds(s0, t), :], rcv_ref[pl.ds(r0, t), :]], axis=0)
        pre = dot(oh, both) + bias
        sig = sigmoid(pre)
        act = (pre * sig).astype(bf16)
        slope_ref[b] = (sig * (1.0 + pre * (1.0 - sig))).astype(bf16)
        ends = ends_ref[b]
        mask = mask_ref[pl.ds(b, 1), :]
        scat = ((ends[1:2, :] == sub) & (mask > 0)).astype(bf16)
        sum_ref[pl.ds(r0, t), :] += dot(scat, act)


def edge_backward(st, rt, cols_ref, ends_ref, g_ref, slope_ref, src_ref, dst_ref):
    blocks, _, t = ends_ref.shape
    src_ref[...] = jnp.zeros_like(src_ref)
    dst_ref[...] = jnp.zeros_like(dst_ref)
    lane = lax.broadcasted_iota(jnp.int32, (t, t), 1)
    sub = lax.broadcasted_iota(jnp.int32, (t, t), 0)

    @pl.loop(0, blocks, unroll=4)
    def _(b):
        cols = cols_ref[b]
        s0 = pl.multiple_of(st[b] * t, t)
        r0 = pl.multiple_of(rt[b] * t, t)
        oh = ((cols[:, 1:2] == lane) & (cols[:, 2:3] > 0)).astype(bf16)
        cot = dot(oh, g_ref[pl.ds(r0, t), :])
        pc = (cot * slope_ref[b].astype(f32)).astype(bf16)
        ends = ends_ref[b]
        src_ref[pl.ds(s0, t), :] += dot((ends[0:1, :] == sub).astype(bf16), pc)
        dst_ref[pl.ds(r0, t), :] += dot((ends[1:2, :] == sub).astype(bf16), pc)


def node_kernel(
    lat_ref, s_ref, wm_ref, wmf_ref, wself_ref, wagg_ref, waggf_ref, bias_ref, wn_ref, wnf_ref,
    gain_ref, cot_ref,
    new_ref, g_ref, grads_ref, lpart_ref, stat_ref,
    sfull, afull, nfull, ssem, rsem,
):
    lat = lax.axis_index("lat")
    other = {"lat": 1 - lat}
    part = s_ref.shape[1]

    def swap(buf, k):
        return remote(buf.at[lat], buf.at[lat], ssem.at[k], rsem.at[k], other)

    def both(buf):
        return jnp.concatenate([buf[0], buf[1]], axis=1)

    enter(1, True)
    sb = s_ref[...].astype(bf16)
    sfull[lat] = sb
    c = swap(sfull, 0)
    c.start()
    latents = lat_ref[...]
    nself = dot(latents, wself_ref[...]) + bias_ref[...]
    c.wait()
    agg = dot(both(sfull), wmf_ref[...]).astype(bf16)
    node_pre = nself + dot(agg, wagg_ref[...])
    sig = sigmoid(node_pre)
    act = (node_pre * sig).astype(bf16)
    afull[lat] = act
    c = swap(afull, 1)
    c.start()
    slope = sig * (1.0 + node_pre * (1.0 - sig))
    c.wait()
    node_out = dot(both(afull), wnf_ref[...])
    mean = jnp.mean(node_out, axis=-1, keepdims=True)
    cen = node_out - mean
    var = jnp.mean(cen * cen, axis=-1, keepdims=True)
    inv = lax.rsqrt(var + norm_eps)
    normed = cen * inv
    gain = gain_ref[...]
    new_ref[...] = (latents.astype(f32) + normed * gain).astype(bf16)
    go = cot_ref[...].astype(f32)
    dn = go * gain
    oc = inv * (
        dn
        - jnp.mean(dn, axis=-1, keepdims=True)
        - normed * jnp.mean(dn * normed, axis=-1, keepdims=True)
    )
    ocb = oc.astype(bf16)
    npc = dot_nt(ocb, wn_ref[...]) * slope
    npb = npc.astype(bf16)
    nfull[lat] = npb
    c = swap(nfull, 2)
    c.start()
    gain_sum = jnp.sum(go * normed, axis=0, keepdims=True)
    stat_ref[0:1, :] = jnp.zeros((1, part), f32)
    stat_ref[1:2, :] = jnp.sum(npc, axis=0, keepdims=True)
    stat_ref[2:3, :] = gain_sum[:, :part]
    stat_ref[3:4, :] = gain_sum[:, part:]
    stat_ref[4:8, :] = jnp.zeros((4, part), f32)
    nw = dot_tn(act, ocb).astype(bf16)
    grads_ref[0:part, :] = nw[:, :part]
    grads_ref[part : 2 * part, :] = nw[:, part:]
    width = latents.shape[1]
    grads_ref[4 * part : 4 * part + width, :] = dot_tn(latents, npb).astype(bf16)
    grads_ref[4 * part + width : 4 * part + 2 * width, :] = dot_tn(agg, npb).astype(bf16)
    lpart_ref[...] = dot_nt(npb, wself_ref[...])
    c.wait()
    ac = dot_nt(both(nfull), waggf_ref[...]).astype(bf16)
    g_ref[...] = dot_nt(ac, wm_ref[...]).astype(bf16)
    mw = dot_tn(sb, ac).astype(bf16)
    grads_ref[2 * part : 3 * part, :] = mw[:, :part]
    grads_ref[3 * part : 4 * part, :] = mw[:, part:]


def back_kernel(
    n, list_ref, ids_ref, lat_ref, src_ref, dst_ref, lpart_ref, ws_ref, wr_ref, cot_ref, stat_in,
    gl_ref, grads_ref, stat_ref,
    hs, hr, pr, own, lps, lsend, lrecv, ssem, rsem, csend, crecv,
):
    me = lax.axis_index("pix")
    lat = lax.axis_index("lat")
    right = lax.rem(me + 1, n)
    left = lax.rem(me + n - 1, n)
    rows, width = lat_ref.shape
    hrows = hs.shape[1]
    crows = pr.shape[1]
    part = src_ref.shape[1]
    base = rows + 2 * hrows
    hs[0] = src_ref[rows : rows + hrows, :].astype(bf16)
    hs[1] = src_ref[rows + hrows : base, :].astype(bf16)
    enter(n, True)
    copies = [
        remote(hs.at[0], hr.at[0], ssem.at[0], rsem.at[0], {"pix": left}),
        remote(hs.at[1], hr.at[1], ssem.at[1], rsem.at[1], {"pix": right}),
    ]
    for d in range(1, n):
        to = lax.rem(me + d, n)
        at = pl.multiple_of(base + to * crows, 8)
        copies.append(
            remote(src_ref.at[pl.ds(at, crows), :], pr.at[me], csend.at[d], crecv.at[d], {"pix": to})
        )
    for c in copies:
        c.start()
    pr[me] = src_ref[pl.ds(pl.multiple_of(base + me * crows, 8), crows), :]
    latents = lat_ref[...]
    dst = dst_ref[...]
    stat_ref[...] = stat_in[...]
    stat_ref[0:1, :] = jnp.sum(dst, axis=0, keepdims=True)
    dstb = dst.astype(bf16)
    grads_ref[width : 2 * width, :] = dot_tn(latents, dstb).astype(bf16)
    lp = lpart_ref[...] + dot_nt(dstb, wr_ref[...])
    for c in copies:
        c.wait()
    slots = list_ref.shape[0]
    t = hrows // slots
    back = hr[0].astype(f32) + hr[1].astype(f32)
    coarse = jnp.sum(pr[...], axis=0)
    sub = lax.broadcasted_iota(jnp.int32, (t, part), 0)
    for tile in range(rows // t):
        v = src_ref[tile * t : (tile + 1) * t, :]
        for k in range(slots):
            hit = jnp.full((t, part), list_ref[k], jnp.int32) == tile
            v = v + jnp.where(hit, back[k * t : (k + 1) * t, :], 0.0)
        for j in range(crows):
            hit = sub == (ids_ref[j] - tile * t)
            v = v + jnp.where(hit, coarse[j : j + 1, :], 0.0)
        own[tile * t : (tile + 1) * t, :] = v.astype(bf16)
    srcb = own[...]
    lp = lp + dot_nt(srcb, ws_ref[...])
    for k in range(2):
        half = lp[:, k * (width // 2) : (k + 1) * (width // 2)]
        lps[k] = half + cot_ref[:, k * (width // 2) : (k + 1) * (width // 2)].astype(f32)
        lsend[k] = half.astype(bf16)
    c = remote(lsend.at[1 - lat], lrecv, ssem.at[2], rsem.at[2], {"lat": 1 - lat})
    c.start()
    grads_ref[0:width, :] = dot_tn(latents, srcb).astype(bf16)
    c.wait()
    gl_ref[...] = lps[lat] + lrecv[...].astype(f32)


def reduce_kernel(
    n, scale, g_ref, stat_in, out_ref, stat_ref,
    r1, s2, r2, gathered, stats,
    p1s, p1r, l1s, l1r, l2s, l2r, p2s, p2r, ts, tr,
):
    me = lax.axis_index("pix")
    q = lax.rem(me, PLANE)
    z = me // PLANE
    m = n // PLANE
    enter(n, False)

    def plane(d):
        return {"pix": z * PLANE + lax.rem(q + d, PLANE)}

    def line(d):
        return {"pix": lax.rem(z + d, m) * PLANE + q}

    first, tiny = [], []
    for g in range(GROUPS):
        cs = []
        for d in range(1, PLANE):
            to = lax.rem(q + d, PLANE)
            cs.append(
                remote(g_ref.at[g, to], r1.at[g, d - 1], p1s.at[g, d - 1], p1r.at[g, d - 1], plane(d))
            )
            cs[-1].start()
        first.append(cs)
    for d in range(1, n):
        c = remote(stat_in, stats.at[me], ts.at[d], tr.at[d], {"pix": lax.rem(me + d, n)})
        c.start()
        tiny.append(c)
    stats[me] = stat_in[...]
    second = []
    for g in range(GROUPS):
        for c in first[g]:
            c.wait()
        acc = g_ref[g, q].astype(f32)
        for k in range(PLANE - 1):
            acc = acc + r1[g, k].astype(f32)
        s2[g] = acc.astype(bf16)
        cs = []
        for d in range(1, m):
            to = lax.rem(z + d, m)
            cs.append(remote(s2.at[g, to], r2.at[g, d - 1], l1s.at[g, d - 1], l1r.at[g, d - 1], line(d)))
            cs[-1].start()
        second.append(cs)
    third = []
    for g in range(GROUPS):
        for c in second[g]:
            c.wait()
        acc = s2[g, z].astype(f32)
        for k in range(m - 1):
            acc = acc + r2[g, k].astype(f32)
        gathered[g, q, z] = acc.astype(bf16)
        cs = []
        for d in range(1, m):
            ref = gathered.at[g, q, z]
            cs.append(remote(ref, ref, l2s.at[g, d - 1], l2r.at[g, d - 1], line(d)))
            cs[-1].start()
        third.append(cs)
    fourth = []
    for g in range(GROUPS):
        for c in third[g]:
            c.wait()
        cs = []
        for d in range(1, PLANE):
            ref = gathered.at[g, q]
            cs.append(remote(ref, ref, p2s.at[g, d - 1], p2r.at[g, d - 1], plane(d)))
            cs[-1].start()
        fourth.append(cs)
    for c in tiny:
        c.wait()
    stat_ref[...] = jnp.sum(stats[...], axis=0) * scale
    for g in range(GROUPS):
        for c in fourth[g]:
            c.wait()
        out_ref[g] = gathered[g].astype(f32) * scale


def shards(
    latents, w_send, w_recv, edge_bias, w_msg, w_self, w_agg, node_bias, w_node, norm_gain,
    coarse_ids, send_list, recv_tile, send_tile, edge_ends, edge_mask, cotangent,
):
    rows, width = latents.shape
    blocks, _, t = edge_ends.shape
    part = w_send.shape[1]
    n = lax.axis_size("pix")
    m = n // PLANE
    slots = send_list.shape[0]
    hrows = slots * t
    crows = coarse_ids.shape[0]
    srows = rows + 2 * hrows + n * crows
    dma = pltpu.SemaphoreType.DMA
    sds = jax.ShapeDtypeStruct
    scale = 1.0 / math.sqrt(rows * n)
    cols = jnp.stack([edge_ends[:, 0], edge_ends[:, 1], edge_mask], axis=-1)
    lent = latents.reshape(rows // t, t, width)[send_list].reshape(hrows, width)
    coarse = latents[coarse_ids]
    src, rcv, wmf, wnf, waf = comm_call(
        functools.partial(share_kernel, n),
        [
            sds((srows, part), bf16), sds((rows, part), bf16), sds((2 * part, width), bf16),
            sds((2 * part, width), bf16), sds((width, 2 * part), bf16),
        ],
        [VM] * 8,
        [
            pltpu.VMEM((2, hrows, width), bf16), pltpu.VMEM((n, crows, width), bf16),
            pltpu.VMEM((2, part, width), bf16), pltpu.VMEM((2, part, width), bf16),
            pltpu.VMEM((2, width, part), bf16), dma((5,)), dma((5,)), dma((n,)), dma((n,)),
        ],
        1,
    )(latents, lent, coarse, w_send, w_recv, w_msg, w_node, w_agg)
    params = pltpu.CompilerParams(vmem_limit_bytes=LIMIT)
    cost = pl.CostEstimate(flops=10**9, bytes_accessed=10**6, transcendentals=0)
    sums, slope = pl.pallas_call(
        edge_forward,
        out_shape=[sds((rows, part), f32), sds((blocks, t, part), bf16)],
        in_specs=[SM, SM] + [VM] * 6,
        out_specs=[VM, VM],
        compiler_params=params,
        cost_estimate=cost,
    )(send_tile, recv_tile, cols, edge_ends, edge_mask, src, rcv, edge_bias[None])
    new, g, grads1, lpart, stat1 = comm_call(
        node_kernel,
        [
            sds((rows, width), bf16), sds((rows, part), bf16), sds((4 * part + 2 * width, part), bf16),
            sds((rows, width), f32), sds((8, part), f32),
        ],
        [VM] * 12,
        [pltpu.VMEM((2, rows, part), bf16)] * 3 + [dma((3,)), dma((3,))],
        2,
    )(
        latents, sums, w_msg, wmf, w_self, w_agg, waf, node_bias[None], w_node, wnf,
        norm_gain[None], cotangent,
    )
    src_cot, dst_cot = pl.pallas_call(
        edge_backward,
        out_shape=[sds((srows, part), f32), sds((rows, part), f32)],
        in_specs=[SM, SM] + [VM] * 4,
        out_specs=[VM, VM],
        compiler_params=params,
        cost_estimate=cost,
    )(send_tile, recv_tile, cols, edge_ends, g, slope)
    gl, grads2, stat2 = comm_call(
        functools.partial(back_kernel, n),
        [sds((rows, width // 2), f32), sds((2 * width, part), bf16), sds((8, part), f32)],
        [SM, SM] + [VM] * 8,
        [
            pltpu.VMEM((2, hrows, part), bf16), pltpu.VMEM((2, hrows, part), bf16),
            pltpu.VMEM((n, crows, part), f32), pltpu.VMEM((rows, part), bf16),
            pltpu.VMEM((2, rows, width // 2), f32), pltpu.VMEM((2, rows, width // 2), bf16),
            pltpu.VMEM((rows, width // 2), bf16), dma((3,)), dma((3,)), dma((n,)), dma((n,)),
        ],
        3,
    )(send_list, coarse_ids, latents, src_cot, dst_cot, lpart, w_send, w_recv, cotangent, stat1)
    grads = jnp.concatenate([grads1, grads2], axis=0)
    per = grads.shape[0] // (GROUPS * n)
    shape = (GROUPS, PLANE, m, per, part)
    total, stat = comm_call(
        functools.partial(reduce_kernel, n, scale),
        [sds(shape, f32), sds((8, part), f32)],
        [VM, VM],
        [
            pltpu.VMEM((GROUPS, PLANE - 1, m, per, part), bf16),
            pltpu.VMEM((GROUPS, m, per, part), bf16),
            pltpu.VMEM((GROUPS, m - 1, per, part), bf16),
            pltpu.VMEM(shape, bf16),
            pltpu.VMEM((n, 8, part), f32),
            dma((GROUPS, PLANE - 1)), dma((GROUPS, PLANE - 1)),
            dma((GROUPS, m - 1)), dma((GROUPS, m - 1)),
            dma((GROUPS, m - 1)), dma((GROUPS, m - 1)),
            dma((GROUPS, PLANE - 1)), dma((GROUPS, PLANE - 1)),
            dma((n,)), dma((n,)),
        ],
        4,
    )(grads.reshape(shape), stat2)
    flat = total.reshape(grads.shape)

    def wide(at):
        return jnp.concatenate([flat[at : at + part], flat[at + part : at + 2 * part]], axis=1)

    a = 4 * part
    return (
        new,
        gl,
        flat[a + 2 * width : a + 3 * width],
        flat[a + 3 * width : a + 4 * width],
        stat[0],
        wide(2 * part),
        flat[a : a + width],
        flat[a + width : a + 2 * width],
        stat[1],
        wide(0),
        jnp.concatenate([stat[2], stat[3]]),
    )


def solution(mesh):
    return jax.shard_map(
        shards,
        mesh=mesh,
        in_specs=(
            P("pix", None), P(None, "lat"), P(None, "lat"), P("lat"), P("lat", None),
            P(None, "lat"), P(None, "lat"), P("lat"), P("lat", None), P(), P("pix"), P("pix"),
            P("pix"), P("pix"), P("pix", None, None), P("pix", None), P("pix", None),
        ),
        out_specs=(
            P("pix", None), P("pix", "lat"), P(None, "lat"), P(None, "lat"), P("lat"),
            P("lat", None), P(None, "lat"), P(None, "lat"), P("lat"), P("lat", None), P(),
        ),
        check_vma=False,
    )
```

```python
import functools
import math

import jax
import jax.numpy as jnp
from jax import lax
from jax.experimental import pallas as pl
from jax.experimental.pallas import tpu as pltpu
from jax.sharding import PartitionSpec as P

norm_eps = 1e-05
f32 = jnp.float32
bf16 = jnp.bfloat16
MESH = pl.DeviceIdType.MESH
VM = pl.BlockSpec(memory_space=pltpu.VMEM)
SM = pl.BlockSpec(memory_space=pltpu.SMEM)
PLANE = 4
GROUPS = 3
CHUNK = 4
LIMIT = 60 * 1024 * 1024


def dot(a, b):
    return jnp.dot(a, b, preferred_element_type=f32)


def dot_tn(a, b):
    return lax.dot_general(a, b, (((0,), (0,)), ((), ())), preferred_element_type=f32)


def dot_nt(a, b):
    return lax.dot_general(a, b, (((1,), (1,)), ((), ())), preferred_element_type=f32)


def sigmoid(v):
    return 0.5 * jnp.tanh(0.5 * v) + 0.5


def remote(src, dst, send, recv, where):
    return pltpu.make_async_remote_copy(
        src_ref=src, dst_ref=dst, send_sem=send, recv_sem=recv, device_id=where, device_id_type=MESH
    )


def enter(pix_count, partner):
    me = lax.axis_index("pix")
    barrier = pltpu.get_barrier_semaphore()
    total = 0
    for d in range(1, pix_count):
        to = lax.rem(me + d, pix_count)
        pl.semaphore_signal(barrier, inc=1, device_id={"pix": to}, device_id_type=MESH)
        total += 1
    if partner:
        other = 1 - lax.axis_index("lat")
        pl.semaphore_signal(barrier, inc=1, device_id={"lat": other}, device_id_type=MESH)
        total += 1
    pl.semaphore_wait(barrier, total)


def step_kernel(
    n, scale,
    list_ref, ids_ref, st, rt,
    lat_ref, ws_ref, wr_ref, ebias_ref, wm_ref, wself_ref, wagg_ref, nbias_ref, wn_ref, gain_ref,
    ends_ref, mask_ref, cot_ref,
    new_ref, gl_ref, gsend_ref, grecv_ref, gmsg_ref, gself_ref, gagg_ref, gnode_ref, stat_ref,
    lent, halo, mine, panel, wm, wn, wa, src_hi, src_lo, rcv_hi, rcv_lo,
    slope_ref, edge_buf, sums, sfull, afull, nfull, g_ref, src_cot, dst_cot,
    hs, hr, pr, own, lps, lsend, lrecv,
    grads, r1, s2, r2, gathered, stat_own, stats,
    ssem, rsem, csend, crecv, bsend, brecv, ts, tr,
    p1s, p1r, l1s, l1r, l2s, l2r, p2s, p2r,
):
    me = lax.axis_index("pix")
    lat = lax.axis_index("lat")
    other = {"lat": 1 - lat}
    right = lax.rem(me + 1, n)
    left = lax.rem(me + n - 1, n)
    q = lax.rem(me, PLANE)
    z = me // PLANE
    m = n // PLANE
    rows, width = lat_ref.shape
    part = ws_ref.shape[1]
    blocks, _, t = ends_ref.shape
    hrows = hs.shape[1]
    crows = pr.shape[1]
    slots = hrows // t
    base = rows + 2 * hrows
    prows = n * crows
    srows = base + prows
    per = grads.shape[3]

    def swap(buf, k):
        return remote(buf.at[lat], buf.at[lat], ssem.at[k], rsem.at[k], other)

    def plane(d):
        return {"pix": z * PLANE + lax.rem(q + d, PLANE)}

    def line(d):
        return {"pix": lax.rem(z + d, m) * PLANE + q}

    def both(buf):
        return jnp.concatenate([buf[0], buf[1]], axis=1)

    def put_grad(g, slot, value):
        count = value.shape[0] // (m * per)
        grads[g, slot : slot + count] = value.reshape(count, m, per, part).astype(bf16)

    def put_wide(g, slot, value):
        put_grad(g, slot, value[:, :part])
        put_grad(g, slot + 1, value[:, part:])

    def reduce_plane(g):
        cs = []
        for d in range(1, PLANE):
            to = lax.rem(q + d, PLANE)
            cs.append(
                remote(grads.at[g, to], r1.at[g, d - 1], p1s.at[g, d - 1], p1r.at[g, d - 1], plane(d))
            )
            cs[-1].start()
        return cs

    def reduce_line(g, before):
        for c in before:
            c.wait()
        acc = grads[g, q].astype(f32)
        for k in range(PLANE - 1):
            acc = acc + r1[g, k].astype(f32)
        s2[g] = acc.astype(bf16)
        cs = []
        for d in range(1, m):
            to = lax.rem(z + d, m)
            cs.append(remote(s2.at[g, to], r2.at[g, d - 1], l1s.at[g, d - 1], l1r.at[g, d - 1], line(d)))
            cs[-1].start()
        return cs

    def gather_line(g, before):
        for c in before:
            c.wait()
        acc = s2[g, z].astype(f32)
        for k in range(m - 1):
            acc = acc + r2[g, k].astype(f32)
        gathered[g, q, z] = acc.astype(bf16)
        ref = gathered.at[g, q, z]
        cs = []
        for d in range(1, m):
            cs.append(remote(ref, ref, l2s.at[g, d - 1], l2r.at[g, d - 1], line(d)))
            cs[-1].start()
        return cs

    def gather_plane(g, before):
        for c in before:
            c.wait()
        ref = gathered.at[g, q]
        cs = []
        for d in range(1, PLANE):
            cs.append(remote(ref, ref, p2s.at[g, d - 1], p2r.at[g, d - 1], plane(d)))
            cs[-1].start()
        return cs

    def taken(g, before, wide_ref, tall_ref, tall_first):
        for c in before:
            c.wait()
        full = (gathered[g].astype(f32) * scale).reshape(PLANE * m * per, part)
        if tall_first:
            wide_ref[...] = full[: 2 * part]
        else:
            wide_ref[:, :part] = full[:part]
            wide_ref[:, part:] = full[part : 2 * part]
        tall_ref[...] = full[2 * part :]

    enter(n, True)
    lrow = lax.broadcasted_iota(jnp.int32, (t, rows), 0)
    lcol = lax.broadcasted_iota(jnp.int32, (t, rows), 1)
    for k in range(slots):
        take = (lcol == lrow + list_ref[k] * t).astype(bf16)
        lent[k * t : (k + 1) * t, :] = dot(take, lat_ref[...]).astype(bf16)
    crow = lax.broadcasted_iota(jnp.int32, (crows, rows), 0)
    ccol = lax.broadcasted_iota(jnp.int32, (crows, rows), 1)
    pick = jnp.zeros((crows, rows), f32)
    for j in range(crows):
        pick = pick + jnp.where((crow == j) & (ccol == ids_ref[j]), 1.0, 0.0)
    mine[...] = dot(pick.astype(bf16), lat_ref[...]).astype(bf16)
    copies = [
        remote(lent, halo.at[0], ssem.at[0], rsem.at[0], {"pix": right}),
        remote(lent, halo.at[1], ssem.at[1], rsem.at[1], {"pix": left}),
    ]
    for d in range(1, n):
        to = lax.rem(me + d, n)
        copies.append(remote(mine, panel.at[me], csend.at[d], crecv.at[d], {"pix": to}))
    wcopies = [
        remote(wm_ref, wm.at[lat], ssem.at[2], rsem.at[2], other),
        remote(wn_ref, wn.at[lat], ssem.at[3], rsem.at[3], other),
        remote(wagg_ref, wa.at[lat], ssem.at[4], rsem.at[4], other),
    ]
    for c in copies + wcopies:
        c.start()
    panel[me] = mine[...]
    wm[lat] = wm_ref[...]
    wn[lat] = wn_ref[...]
    wa[lat] = wagg_ref[...]

    def split(hi, lo, at, value):
        top = value.astype(bf16)
        rest = (value - top.astype(f32)).astype(bf16)
        for k in range(value.shape[0] // t):
            hi[at // t + k] = top[k * t : (k + 1) * t, :]
            lo[at // t + k] = rest[k * t : (k + 1) * t, :]

    split(src_hi, src_lo, 0, dot(lat_ref[...], ws_ref[...]))
    split(rcv_hi, rcv_lo, 0, dot(lat_ref[...], wr_ref[...]))
    nself = dot(lat_ref[...], wself_ref[...]) + nbias_ref[...]
    for c in copies:
        c.wait()
    for k in range(2):
        split(src_hi, src_lo, rows + k * hrows, dot(halo[k], ws_ref[...]))
    flat = panel[...].astype(f32).reshape(prows, width).astype(bf16)
    split(src_hi, src_lo, base, dot(flat, ws_ref[...]))

    sub = lax.broadcasted_iota(jnp.int32, (t, t), 0)
    ebias = ebias_ref[...]

    @pl.loop(0, blocks, unroll=4)
    def _(b):
        ends = ends_ref[b]
        oh_s = (ends[0:1, :] == sub).astype(bf16)
        oh_r = (ends[1:2, :] == sub).astype(bf16)
        oh = jnp.concatenate([oh_s, oh_r, oh_s, oh_r], axis=0)
        s0 = st[b]
        r0 = rt[b]
        tabs = jnp.concatenate([src_hi[s0], rcv_hi[r0], src_lo[s0], rcv_lo[r0]], axis=0)
        pre = dot_tn(oh, tabs) + ebias
        sig = sigmoid(pre)
        edge_buf[b] = (pre * sig).astype(bf16)
        slope_ref[b] = sig * (1.0 + pre * (1.0 - sig))

    def ids_row(c, end, tile_ref):
        parts = []
        for i in range(CHUNK):
            b = c * CHUNK + i
            parts.append(ends_ref[b][end : end + 1, :] + tile_ref[b] * t)
        return jnp.concatenate(parts, axis=1)

    def edge_rows(c):
        return jnp.concatenate([edge_buf[c * CHUNK + i] for i in range(CHUNK)], axis=0)

    wide_sub = lax.broadcasted_iota(jnp.int32, (rows, CHUNK * t), 0)
    src_sub = lax.broadcasted_iota(jnp.int32, (srows, CHUNK * t), 0)
    sums[...] = jnp.zeros_like(sums)

    @pl.loop(0, blocks // CHUNK)
    def _(c):
        live = jnp.concatenate([mask_ref[pl.ds(c * CHUNK + i, 1), :] for i in range(CHUNK)], axis=1)
        goal = jnp.where(live > 0, ids_row(c, 1, rt), -1)
        sums[...] += dot((wide_sub == goal).astype(bf16), edge_rows(c))

    sb = sums[...].astype(bf16)
    sfull[lat] = sb
    cs = swap(sfull, 5)
    cs.start()
    for c in wcopies:
        c.wait()
    wmf = jnp.concatenate([wm[0], wm[1]], axis=0)
    cs.wait()
    agg = dot(both(sfull), wmf).astype(bf16)
    node_pre = nself + dot(agg, wagg_ref[...])
    sig = sigmoid(node_pre)
    act = (node_pre * sig).astype(bf16)
    afull[lat] = act
    cs = swap(afull, 6)
    cs.start()
    slope = sig * (1.0 + node_pre * (1.0 - sig))
    wnf = jnp.concatenate([wn[0], wn[1]], axis=0)
    cs.wait()
    node_out = dot(both(afull), wnf)
    mean = jnp.mean(node_out, axis=-1, keepdims=True)
    cen = node_out - mean
    var = jnp.mean(cen * cen, axis=-1, keepdims=True)
    inv = lax.rsqrt(var + norm_eps)
    normed = cen * inv
    gain = gain_ref[...]
    new_ref[...] = (lat_ref[...].astype(f32) + normed * gain).astype(bf16)
    go = cot_ref[...].astype(f32)
    dn = go * gain
    oc = inv * (
        dn
        - jnp.mean(dn, axis=-1, keepdims=True)
        - normed * jnp.mean(dn * normed, axis=-1, keepdims=True)
    )
    ocb = oc.astype(bf16)
    npc = dot_nt(ocb, wn_ref[...]) * slope
    npb = npc.astype(bf16)
    nfull[lat] = npb
    cs = swap(nfull, 7)
    cs.start()
    put_wide(0, 0, dot_tn(act, ocb))
    put_grad(0, 2, dot_tn(lat_ref[...], npb))
    a0 = reduce_plane(0)
    gain_sum = jnp.sum(go * normed, axis=0, keepdims=True)
    stat_own[1:2, :] = jnp.sum(npc, axis=0, keepdims=True)
    stat_own[2:3, :] = gain_sum[:, :part]
    stat_own[3:4, :] = gain_sum[:, part:]
    stat_own[4:8, :] = jnp.zeros((4, part), f32)
    cs.wait()
    ac = dot_nt(both(nfull), both(wa)).astype(bf16)
    back_part = dot_nt(ac, wm_ref[...]).astype(bf16)
    for k in range(rows // t):
        g_ref[k] = back_part[k * t : (k + 1) * t, :]
    put_wide(1, 0, dot_tn(sb, ac))
    put_grad(1, 2, dot_tn(agg, npb))
    a1 = reduce_plane(1)

    @pl.loop(0, blocks, unroll=4)
    def _(b):
        ends = ends_ref[b]
        r0 = rt[b]
        oh = ((ends[1:2, :] == sub) & (mask_ref[pl.ds(b, 1), :] > 0)).astype(bf16)
        edge_buf[b] = (dot_tn(oh, g_ref[r0]) * slope_ref[b]).astype(bf16)

    src_cot[...] = jnp.zeros_like(src_cot)

    @pl.loop(0, blocks // CHUNK)
    def _(c):
        src_cot[...] += dot((src_sub == ids_row(c, 0, st)).astype(bf16), edge_rows(c))

    hs[0] = src_cot[rows : rows + hrows, :].astype(bf16)
    hs[1] = src_cot[rows + hrows : base, :].astype(bf16)
    copies = [
        remote(hs.at[0], hr.at[0], ssem.at[8], rsem.at[8], {"pix": left}),
        remote(hs.at[1], hr.at[1], ssem.at[9], rsem.at[9], {"pix": right}),
    ]
    for d in range(1, n):
        to = lax.rem(me + d, n)
        at = pl.multiple_of(base + to * crows, 8)
        copies.append(
            remote(src_cot.at[pl.ds(at, crows), :], pr.at[me], bsend.at[d], brecv.at[d], {"pix": to})
        )
    for c in copies:
        c.start()
    pr[me] = src_cot[pl.ds(pl.multiple_of(base + me * crows, 8), crows), :]
    a0 = reduce_line(0, a0)
    dst_cot[...] = jnp.zeros_like(dst_cot)

    @pl.loop(0, blocks // CHUNK)
    def _(c):
        dst_cot[...] += dot((wide_sub == ids_row(c, 1, rt)).astype(bf16), edge_rows(c))

    dst = dst_cot[...]
    stat_own[0:1, :] = jnp.sum(dst, axis=0, keepdims=True)
    tiny = []
    for d in range(1, n):
        c = remote(stat_own, stats.at[me], ts.at[d], tr.at[d], {"pix": lax.rem(me + d, n)})
        c.start()
        tiny.append(c)
    stats[me] = stat_own[...]
    dstb = dst.astype(bf16)
    a1 = reduce_line(1, a1)
    a0 = gather_line(0, a0)
    for c in copies:
        c.wait()
    back = hr[0].astype(f32) + hr[1].astype(f32)
    coarse = jnp.sum(pr[...], axis=0)
    tsub = lax.broadcasted_iota(jnp.int32, (t, part), 0)
    for tile in range(rows // t):
        v = src_cot[tile * t : (tile + 1) * t, :]
        for k in range(slots):
            hit = jnp.full((t, part), list_ref[k], jnp.int32) == tile
            v = v + jnp.where(hit, back[k * t : (k + 1) * t, :], 0.0)
        for j in range(crows):
            v = v + jnp.where(tsub == (ids_ref[j] - tile * t), coarse[j : j + 1, :], 0.0)
        own[tile * t : (tile + 1) * t, :] = v.astype(bf16)
    srcb = own[...]
    put_grad(2, 0, dot_tn(lat_ref[...], srcb))
    put_grad(2, 2, dot_tn(lat_ref[...], dstb))
    a2 = reduce_plane(2)
    lp = dot_nt(npb, wself_ref[...]) + dot_nt(dstb, wr_ref[...]) + dot_nt(srcb, ws_ref[...])
    half = width // 2
    for k in range(2):
        piece = lp[:, k * half : (k + 1) * half]
        lps[k] = piece + cot_ref[:, k * half : (k + 1) * half].astype(f32)
        lsend[k] = piece.astype(bf16)
    cs = remote(lsend.at[1 - lat], lrecv, ssem.at[10], rsem.at[10], other)
    cs.start()
    a0 = gather_plane(0, a0)
    a1 = gather_line(1, a1)
    cs.wait()
    gl_ref[...] = lps[lat] + lrecv[...].astype(f32)
    a1 = gather_plane(1, a1)
    a2 = reduce_line(2, a2)
    for c in tiny:
        c.wait()
    stat_ref[...] = jnp.sum(stats[...], axis=0) * scale
    a2 = gather_line(2, a2)
    taken(0, a0, gnode_ref, gself_ref, False)
    a2 = gather_plane(2, a2)
    taken(1, a1, gmsg_ref, gagg_ref, False)
    taken(2, a2, gsend_ref, grecv_ref, True)


def shards(
    latents, w_send, w_recv, edge_bias, w_msg, w_self, w_agg, node_bias, w_node, norm_gain,
    coarse_ids, send_list, recv_tile, send_tile, edge_ends, edge_mask, cotangent,
):
    rows, width = latents.shape
    blocks, _, t = edge_ends.shape
    part = w_send.shape[1]
    n = lax.axis_size("pix")
    m = n // PLANE
    hrows = send_list.shape[0] * t
    crows = coarse_ids.shape[0]
    srows = rows + 2 * hrows + n * crows
    per = 4 * part // n
    half = width // 2
    dma = pltpu.SemaphoreType.DMA
    sds = jax.ShapeDtypeStruct
    V = pltpu.VMEM
    scale = 1.0 / math.sqrt(rows * n)
    tall = sds((width, part), f32)
    broad = sds((part, width), f32)
    outs = [sds((rows, width), bf16), sds((rows, half), f32), tall, tall, broad, tall, tall, broad, sds((8, part), f32)]
    line_sems = [dma((GROUPS, m - 1))] * 4
    plane_sems = [dma((GROUPS, PLANE - 1))] * 2
    res = pl.pallas_call(
        functools.partial(step_kernel, n, scale),
        out_shape=outs,
        in_specs=[SM] * 4 + [VM] * 13,
        out_specs=[VM] * len(outs),
        scratch_shapes=[
            V((hrows, width), bf16), V((2, hrows, width), bf16),
            V((crows, width), bf16), V((n, crows, width), bf16),
            V((2, part, width), bf16), V((2, part, width), bf16), V((2, width, part), bf16),
            V((srows // t, t, part), bf16), V((srows // t, t, part), bf16), V((rows // t, t, part), bf16), V((rows // t, t, part), bf16),
            V((blocks, t, part), f32), V((blocks, t, part), bf16), V((rows, part), f32),
            V((2, rows, part), bf16), V((2, rows, part), bf16), V((2, rows, part), bf16),
            V((rows // t, t, part), bf16), V((srows, part), f32), V((rows, part), f32),
            V((2, hrows, part), bf16), V((2, hrows, part), bf16), V((n, crows, part), f32),
            V((rows, part), bf16), V((2, rows, half), f32), V((2, rows, half), bf16), V((rows, half), bf16),
            V((GROUPS, PLANE, m, per, part), bf16), V((GROUPS, PLANE - 1, m, per, part), bf16),
            V((GROUPS, m, per, part), bf16), V((GROUPS, m - 1, per, part), bf16),
            V((GROUPS, PLANE, m, per, part), bf16), V((8, part), f32), V((n, 8, part), f32),
            dma((11,)), dma((11,)), dma((n,)), dma((n,)), dma((n,)), dma((n,)), dma((n,)), dma((n,)),
        ] + plane_sems + line_sems + plane_sems,
        compiler_params=pltpu.CompilerParams(
            collective_id=1, has_side_effects=True, vmem_limit_bytes=LIMIT
        ),
    )(
        send_list, coarse_ids, send_tile, recv_tile, latents, w_send, w_recv, edge_bias[None], w_msg,
        w_self, w_agg, node_bias[None], w_node, norm_gain[None], edge_ends, edge_mask, cotangent,
    )
    new, gl, gsend, grecv, gmsg, gself, gagg, gnode, stat = res
    return (
        new, gl, gsend, grecv, stat[0], gmsg, gself, gagg, stat[1], gnode,
        jnp.concatenate([stat[2], stat[3]]),
    )


def solution(mesh):
    return jax.shard_map(
        shards,
        mesh=mesh,
        in_specs=(
            P("pix", None), P(None, "lat"), P(None, "lat"), P("lat"), P("lat", None),
            P(None, "lat"), P(None, "lat"), P("lat"), P("lat", None), P(), P("pix"), P("pix"),
            P("pix"), P("pix"), P("pix", None, None), P("pix", None), P("pix", None),
        ),
        out_specs=(
            P("pix", None), P("pix", "lat"), P(None, "lat"), P(None, "lat"), P("lat"),
            P("lat", None), P(None, "lat"), P(None, "lat"), P("lat"), P("lat", None), P(),
        ),
        check_vma=False,
    )
```

```python
import functools
import math

import jax
import jax.numpy as jnp
from jax import lax
from jax.experimental import pallas as pl
from jax.experimental.pallas import tpu as pltpu
from jax.sharding import PartitionSpec as P

norm_eps = 1e-05
f32 = jnp.float32
bf16 = jnp.bfloat16
MESH = pl.DeviceIdType.MESH
VM = pl.BlockSpec(memory_space=pltpu.VMEM)
SM = pl.BlockSpec(memory_space=pltpu.SMEM)
PLANE = 4
GROUPS = 3
CHUNK = 4
LIMIT = 60 * 1024 * 1024


def dot(a, b):
    return jnp.dot(a, b, preferred_element_type=f32)


def dot_tn(a, b):
    return lax.dot_general(a, b, (((0,), (0,)), ((), ())), preferred_element_type=f32)


def dot_nt(a, b):
    return lax.dot_general(a, b, (((1,), (1,)), ((), ())), preferred_element_type=f32)


def sigmoid(v):
    return 0.5 * jnp.tanh(0.5 * v) + 0.5


def remote(src, dst, send, recv, where):
    return pltpu.make_async_remote_copy(
        src_ref=src, dst_ref=dst, send_sem=send, recv_sem=recv, device_id=where, device_id_type=MESH
    )


def enter(pix_count, partner):
    me = lax.axis_index("pix")
    barrier = pltpu.get_barrier_semaphore()
    total = 0
    for d in range(1, pix_count):
        to = lax.rem(me + d, pix_count)
        pl.semaphore_signal(barrier, inc=1, device_id={"pix": to}, device_id_type=MESH)
        total += 1
    if partner:
        other = 1 - lax.axis_index("lat")
        pl.semaphore_signal(barrier, inc=1, device_id={"lat": other}, device_id_type=MESH)
        total += 1
    pl.semaphore_wait(barrier, total)


def step_kernel(
    n, scale,
    list_ref, ids_ref, st, rt,
    lat_ref, ws_ref, wr_ref, ebias_ref, wm_ref, wself_ref, wagg_ref, nbias_ref, wn_ref, gain_ref,
    ends_ref, mask_ref, cot_ref,
    new_ref, gl_ref, gsend_ref, grecv_ref, gmsg_ref, gself_ref, gagg_ref, gnode_ref, stat_ref,
    lent, halo, mine, panel, wm, wn, wa, src_hi, src_lo, rcv_hi, rcv_lo,
    slope_ref, edge_buf, sums, sfull, afull, nfull, g_ref, src_cot, dst_cot,
    hs, hr, pr, own, lps, lsend, lrecv,
    grads, r1, s2, r2, gathered, stat_own, stats, lat_t,
    ssem, rsem, csend, crecv, bsend, brecv, ts, tr,
    p1s, p1r, l1s, l1r, l2s, l2r, p2s, p2r,
):
    me = lax.axis_index("pix")
    lat = lax.axis_index("lat")
    other = {"lat": 1 - lat}
    right = lax.rem(me + 1, n)
    left = lax.rem(me + n - 1, n)
    q = lax.rem(me, PLANE)
    z = me // PLANE
    m = n // PLANE
    rows, width = lat_ref.shape
    part = ws_ref.shape[1]
    blocks, _, t = ends_ref.shape
    hrows = hs.shape[1]
    crows = pr.shape[1]
    slots = hrows // t
    base = rows + 2 * hrows
    prows = n * crows
    srows = base + prows
    per = grads.shape[3]

    def swap(buf, k):
        return remote(buf.at[lat], buf.at[lat], ssem.at[k], rsem.at[k], other)

    def plane(d):
        return {"pix": z * PLANE + lax.rem(q + d, PLANE)}

    def line(d):
        return {"pix": lax.rem(z + d, m) * PLANE + q}

    def both(buf):
        return jnp.concatenate([buf[0], buf[1]], axis=1)

    def put_grad(g, slot, value):
        count = value.shape[0] // (m * per)
        grads[g, slot : slot + count] = value.reshape(count, m, per, part).astype(bf16)

    def put_wide(g, slot, value):
        put_grad(g, slot, value[:, :part])
        put_grad(g, slot + 1, value[:, part:])

    def reduce_plane(g):
        cs = []
        for d in range(1, PLANE):
            to = lax.rem(q + d, PLANE)
            cs.append(
                remote(grads.at[g, to], r1.at[g, d - 1], p1s.at[g, d - 1], p1r.at[g, d - 1], plane(d))
            )
            cs[-1].start()
        return cs

    def reduce_line(g, before):
        for c in before:
            c.wait()
        acc = grads[g, q].astype(f32)
        for k in range(PLANE - 1):
            acc = acc + r1[g, k].astype(f32)
        s2[g] = acc.astype(bf16)
        cs = []
        for d in range(1, m):
            to = lax.rem(z + d, m)
            cs.append(remote(s2.at[g, to], r2.at[g, d - 1], l1s.at[g, d - 1], l1r.at[g, d - 1], line(d)))
            cs[-1].start()
        return cs

    def gather_line(g, before):
        for c in before:
            c.wait()
        acc = s2[g, z].astype(f32)
        for k in range(m - 1):
            acc = acc + r2[g, k].astype(f32)
        gathered[g, q, z] = acc.astype(bf16)
        ref = gathered.at[g, q, z]
        cs = []
        for d in range(1, m):
            cs.append(remote(ref, ref, l2s.at[g, d - 1], l2r.at[g, d - 1], line(d)))
            cs[-1].start()
        return cs

    def gather_plane(g, before):
        for c in before:
            c.wait()
        ref = gathered.at[g, q]
        cs = []
        for d in range(1, PLANE):
            cs.append(remote(ref, ref, p2s.at[g, d - 1], p2r.at[g, d - 1], plane(d)))
            cs[-1].start()
        return cs

    def taken(g, before, wide_ref, tall_ref, tall_first):
        for c in before:
            c.wait()
        full = (gathered[g].astype(f32) * scale).reshape(PLANE * m * per, part)
        if tall_first:
            wide_ref[...] = full[: 2 * part]
        else:
            wide_ref[:, :part] = full[:part]
            wide_ref[:, part:] = full[part : 2 * part]
        tall_ref[...] = full[2 * part :]

    enter(n, True)
    lrow = lax.broadcasted_iota(jnp.int32, (t, rows), 0)
    lcol = lax.broadcasted_iota(jnp.int32, (t, rows), 1)
    for k in range(slots):
        take = (lcol == lrow + list_ref[k] * t).astype(bf16)
        lent[k * t : (k + 1) * t, :] = dot(take, lat_ref[...]).astype(bf16)
    crow = lax.broadcasted_iota(jnp.int32, (crows, rows), 0)
    ccol = lax.broadcasted_iota(jnp.int32, (crows, rows), 1)
    pick = jnp.zeros((crows, rows), f32)
    for j in range(crows):
        pick = pick + jnp.where((crow == j) & (ccol == ids_ref[j]), 1.0, 0.0)
    mine[...] = dot(pick.astype(bf16), lat_ref[...]).astype(bf16)
    copies = [
        remote(lent, halo.at[0], ssem.at[0], rsem.at[0], {"pix": right}),
        remote(lent, halo.at[1], ssem.at[1], rsem.at[1], {"pix": left}),
    ]
    for d in range(1, n):
        to = lax.rem(me + d, n)
        copies.append(remote(mine, panel.at[me], csend.at[d], crecv.at[d], {"pix": to}))
    wcopies = [
        remote(wm_ref, wm.at[lat], ssem.at[2], rsem.at[2], other),
        remote(wn_ref, wn.at[lat], ssem.at[3], rsem.at[3], other),
        remote(wagg_ref, wa.at[lat], ssem.at[4], rsem.at[4], other),
    ]
    for c in copies + wcopies:
        c.start()
    panel[me] = mine[...]
    wm[lat] = wm_ref[...]
    wn[lat] = wn_ref[...]
    wa[lat] = wagg_ref[...]

    def split(hi, lo, at, value):
        top = value.astype(bf16)
        rest = (value - top.astype(f32)).astype(bf16)
        for k in range(value.shape[0] // t):
            hi[at // t + k] = top[k * t : (k + 1) * t, :]
            lo[at // t + k] = rest[k * t : (k + 1) * t, :]

    split(src_hi, src_lo, 0, dot(lat_ref[...], ws_ref[...]))
    split(rcv_hi, rcv_lo, 0, dot(lat_ref[...], wr_ref[...]))
    nself = dot(lat_ref[...], wself_ref[...]) + nbias_ref[...]
    lat_t[...] = lat_ref[...].T
    for c in copies:
        c.wait()
    for k in range(2):
        split(src_hi, src_lo, rows + k * hrows, dot(halo[k], ws_ref[...]))
    flat = panel[...].astype(f32).reshape(prows, width).astype(bf16)
    split(src_hi, src_lo, base, dot(flat, ws_ref[...]))

    lane = lax.broadcasted_iota(jnp.int32, (t, t), 1)
    ebias = ebias_ref[...]

    @pl.loop(0, blocks, unroll=4)
    def _(b):
        ends = ends_ref[b]
        cols = jnp.concatenate([ends] * 4, axis=0).T
        oh_s = (cols[:, 0:1] == lane).astype(bf16)
        oh_r = (cols[:, 1:2] == lane).astype(bf16)
        oh = jnp.concatenate([oh_s, oh_r, oh_s, oh_r], axis=1)
        s0 = st[b]
        r0 = rt[b]
        tabs = jnp.concatenate([src_hi[s0], rcv_hi[r0], src_lo[s0], rcv_lo[r0]], axis=0)
        pre = dot(oh, tabs) + ebias
        sig = sigmoid(pre)
        edge_buf[b] = (pre * sig).astype(bf16)
        slope_ref[b] = sig * (1.0 + pre * (1.0 - sig))

    def ids_row(c, end, tile_ref):
        parts = []
        for i in range(CHUNK):
            b = c * CHUNK + i
            parts.append(ends_ref[b][end : end + 1, :] + tile_ref[b] * t)
        return jnp.concatenate(parts, axis=1)

    def edge_rows(c):
        return jnp.concatenate([edge_buf[c * CHUNK + i] for i in range(CHUNK)], axis=0)

    wide_sub = lax.broadcasted_iota(jnp.int32, (rows, CHUNK * t), 0)
    src_sub = lax.broadcasted_iota(jnp.int32, (srows, CHUNK * t), 0)
    sums[...] = jnp.zeros_like(sums)

    @pl.loop(0, blocks // CHUNK)
    def _(c):
        live = jnp.concatenate([mask_ref[pl.ds(c * CHUNK + i, 1), :] for i in range(CHUNK)], axis=1)
        goal = jnp.where(live > 0, ids_row(c, 1, rt), -1)
        sums[...] += dot((wide_sub == goal).astype(bf16), edge_rows(c))

    sb = sums[...].astype(bf16)
    sfull[lat] = sb
    cs = swap(sfull, 5)
    cs.start()
    for c in wcopies:
        c.wait()
    wmf = jnp.concatenate([wm[0], wm[1]], axis=0)
    cs.wait()
    agg = dot(both(sfull), wmf).astype(bf16)
    node_pre = nself + dot(agg, wagg_ref[...])
    sig = sigmoid(node_pre)
    act = (node_pre * sig).astype(bf16)
    afull[lat] = act
    cs = swap(afull, 6)
    cs.start()
    slope = sig * (1.0 + node_pre * (1.0 - sig))
    wnf = jnp.concatenate([wn[0], wn[1]], axis=0)
    cs.wait()
    node_out = dot(both(afull), wnf)
    mean = jnp.mean(node_out, axis=-1, keepdims=True)
    cen = node_out - mean
    var = jnp.mean(cen * cen, axis=-1, keepdims=True)
    inv = lax.rsqrt(var + norm_eps)
    normed = cen * inv
    gain = gain_ref[...]
    new_ref[...] = (lat_ref[...].astype(f32) + normed * gain).astype(bf16)
    go = cot_ref[...].astype(f32)
    dn = go * gain
    oc = inv * (
        dn
        - jnp.mean(dn, axis=-1, keepdims=True)
        - normed * jnp.mean(dn * normed, axis=-1, keepdims=True)
    )
    ocb = oc.astype(bf16)
    npc = dot_nt(ocb, wn_ref[...]) * slope
    npb = npc.astype(bf16)
    nfull[lat] = npb
    cs = swap(nfull, 7)
    cs.start()
    put_wide(0, 0, dot_tn(act, ocb))
    put_grad(0, 2, dot(lat_t[...], npb))
    a0 = reduce_plane(0)
    gain_sum = jnp.sum(go * normed, axis=0, keepdims=True)
    stat_own[1:2, :] = jnp.sum(npc, axis=0, keepdims=True)
    stat_own[2:3, :] = gain_sum[:, :part]
    stat_own[3:4, :] = gain_sum[:, part:]
    stat_own[4:8, :] = jnp.zeros((4, part), f32)
    cs.wait()
    ac = dot_nt(both(nfull), both(wa)).astype(bf16)
    back_part = dot_nt(ac, wm_ref[...]).astype(bf16)
    for k in range(rows // t):
        g_ref[k] = back_part[k * t : (k + 1) * t, :]
    put_wide(1, 0, dot_tn(sb, ac))
    put_grad(1, 2, dot_tn(agg, npb))
    a1 = reduce_plane(1)

    @pl.loop(0, blocks, unroll=4)
    def _(b):
        ends = ends_ref[b]
        r0 = rt[b]
        goal = jnp.where(mask_ref[pl.ds(b, 1), :] > 0, ends[1:2, :], -1)
        cols = jnp.concatenate([goal] * 8, axis=0).T
        oh = (cols[:, 0:1] == lane).astype(bf16)
        edge_buf[b] = (dot(oh, g_ref[r0]) * slope_ref[b]).astype(bf16)

    src_cot[...] = jnp.zeros_like(src_cot)

    @pl.loop(0, blocks // CHUNK)
    def _(c):
        src_cot[...] += dot((src_sub == ids_row(c, 0, st)).astype(bf16), edge_rows(c))

    hs[0] = src_cot[rows : rows + hrows, :].astype(bf16)
    hs[1] = src_cot[rows + hrows : base, :].astype(bf16)
    copies = [
        remote(hs.at[0], hr.at[0], ssem.at[8], rsem.at[8], {"pix": left}),
        remote(hs.at[1], hr.at[1], ssem.at[9], rsem.at[9], {"pix": right}),
    ]
    for d in range(1, n):
        to = lax.rem(me + d, n)
        at = pl.multiple_of(base + to * crows, 8)
        copies.append(
            remote(src_cot.at[pl.ds(at, crows), :], pr.at[me], bsend.at[d], brecv.at[d], {"pix": to})
        )
    for c in copies:
        c.start()
    pr[me] = src_cot[pl.ds(pl.multiple_of(base + me * crows, 8), crows), :]
    a0 = reduce_line(0, a0)
    dst_cot[...] = jnp.zeros_like(dst_cot)

    @pl.loop(0, blocks // CHUNK)
    def _(c):
        dst_cot[...] += dot((wide_sub == ids_row(c, 1, rt)).astype(bf16), edge_rows(c))

    dst = dst_cot[...]
    stat_own[0:1, :] = jnp.sum(dst, axis=0, keepdims=True)
    tiny = []
    for d in range(1, n):
        c = remote(stat_own, stats.at[me], ts.at[d], tr.at[d], {"pix": lax.rem(me + d, n)})
        c.start()
        tiny.append(c)
    stats[me] = stat_own[...]
    dstb = dst.astype(bf16)
    put_grad(2, 2, dot(lat_t[...], dstb))
    lp = dot_nt(npb, wself_ref[...]) + dot_nt(dstb, wr_ref[...])
    a1 = reduce_line(1, a1)
    a0 = gather_line(0, a0)
    for c in copies:
        c.wait()
    back = hr[0].astype(f32) + hr[1].astype(f32)
    coarse = jnp.sum(pr[...], axis=0)
    tsub = lax.broadcasted_iota(jnp.int32, (t, part), 0)
    for tile in range(rows // t):
        v = src_cot[tile * t : (tile + 1) * t, :]
        for k in range(slots):
            hit = jnp.full((t, part), list_ref[k], jnp.int32) == tile
            v = v + jnp.where(hit, back[k * t : (k + 1) * t, :], 0.0)
        for j in range(crows):
            v = v + jnp.where(tsub == (ids_ref[j] - tile * t), coarse[j : j + 1, :], 0.0)
        own[tile * t : (tile + 1) * t, :] = v.astype(bf16)
    srcb = own[...]
    put_grad(2, 0, dot(lat_t[...], srcb))
    a2 = reduce_plane(2)
    lp = lp + dot_nt(srcb, ws_ref[...])
    half = width // 2
    for k in range(2):
        piece = lp[:, k * half : (k + 1) * half]
        lps[k] = piece + cot_ref[:, k * half : (k + 1) * half].astype(f32)
        lsend[k] = piece.astype(bf16)
    cs = remote(lsend.at[1 - lat], lrecv, ssem.at[10], rsem.at[10], other)
    cs.start()
    a0 = gather_plane(0, a0)
    a1 = gather_line(1, a1)
    cs.wait()
    gl_ref[...] = lps[lat] + lrecv[...].astype(f32)
    a1 = gather_plane(1, a1)
    a2 = reduce_line(2, a2)
    for c in tiny:
        c.wait()
    stat_ref[...] = jnp.sum(stats[...], axis=0) * scale
    a2 = gather_line(2, a2)
    taken(0, a0, gnode_ref, gself_ref, False)
    a2 = gather_plane(2, a2)
    taken(1, a1, gmsg_ref, gagg_ref, False)
    taken(2, a2, gsend_ref, grecv_ref, True)


def shards(
    latents, w_send, w_recv, edge_bias, w_msg, w_self, w_agg, node_bias, w_node, norm_gain,
    coarse_ids, send_list, recv_tile, send_tile, edge_ends, edge_mask, cotangent,
):
    rows, width = latents.shape
    blocks, _, t = edge_ends.shape
    part = w_send.shape[1]
    n = lax.axis_size("pix")
    m = n // PLANE
    hrows = send_list.shape[0] * t
    crows = coarse_ids.shape[0]
    srows = rows + 2 * hrows + n * crows
    per = 4 * part // n
    half = width // 2
    dma = pltpu.SemaphoreType.DMA
    sds = jax.ShapeDtypeStruct
    V = pltpu.VMEM
    scale = 1.0 / math.sqrt(rows * n)
    tall = sds((width, part), f32)
    broad = sds((part, width), f32)
    outs = [sds((rows, width), bf16), sds((rows, half), f32), tall, tall, broad, tall, tall, broad, sds((8, part), f32)]
    line_sems = [dma((GROUPS, m - 1))] * 4
    plane_sems = [dma((GROUPS, PLANE - 1))] * 2
    res = pl.pallas_call(
        functools.partial(step_kernel, n, scale),
        out_shape=outs,
        in_specs=[SM] * 4 + [VM] * 13,
        out_specs=[VM] * len(outs),
        scratch_shapes=[
            V((hrows, width), bf16), V((2, hrows, width), bf16),
            V((crows, width), bf16), V((n, crows, width), bf16),
            V((2, part, width), bf16), V((2, part, width), bf16), V((2, width, part), bf16),
            V((srows // t, t, part), bf16), V((srows // t, t, part), bf16), V((rows // t, t, part), bf16), V((rows // t, t, part), bf16),
            V((blocks, t, part), f32), V((blocks, t, part), bf16), V((rows, part), f32),
            V((2, rows, part), bf16), V((2, rows, part), bf16), V((2, rows, part), bf16),
            V((rows // t, t, part), bf16), V((srows, part), f32), V((rows, part), f32),
            V((2, hrows, part), bf16), V((2, hrows, part), bf16), V((n, crows, part), f32),
            V((rows, part), bf16), V((2, rows, half), f32), V((2, rows, half), bf16), V((rows, half), bf16),
            V((GROUPS, PLANE, m, per, part), bf16), V((GROUPS, PLANE - 1, m, per, part), bf16),
            V((GROUPS, m, per, part), bf16), V((GROUPS, m - 1, per, part), bf16),
            V((GROUPS, PLANE, m, per, part), bf16), V((8, part), f32), V((n, 8, part), f32), V((width, rows), bf16),
            dma((11,)), dma((11,)), dma((n,)), dma((n,)), dma((n,)), dma((n,)), dma((n,)), dma((n,)),
        ] + plane_sems + line_sems + plane_sems,
        compiler_params=pltpu.CompilerParams(
            collective_id=1, has_side_effects=True, vmem_limit_bytes=LIMIT
        ),
    )(
        send_list, coarse_ids, send_tile, recv_tile, latents, w_send, w_recv, edge_bias[None], w_msg,
        w_self, w_agg, node_bias[None], w_node, norm_gain[None], edge_ends, edge_mask, cotangent,
    )
    new, gl, gsend, grecv, gmsg, gself, gagg, gnode, stat = res
    return (
        new, gl, gsend, grecv, stat[0], gmsg, gself, gagg, stat[1], gnode,
        jnp.concatenate([stat[2], stat[3]]),
    )


def solution(mesh):
    return jax.shard_map(
        shards,
        mesh=mesh,
        in_specs=(
            P("pix", None), P(None, "lat"), P(None, "lat"), P("lat"), P("lat", None),
            P(None, "lat"), P(None, "lat"), P("lat"), P("lat", None), P(), P("pix"), P("pix"),
            P("pix"), P("pix"), P("pix", None, None), P("pix", None), P("pix", None),
        ),
        out_specs=(
            P("pix", None), P("pix", "lat"), P(None, "lat"), P(None, "lat"), P("lat"),
            P("lat", None), P(None, "lat"), P(None, "lat"), P("lat"), P("lat", None), P(),
        ),
        check_vma=False,
    )
```
